32 devices in a mesh: parts: 2 (over x), chol: 16 (over z, y, core).
Axes of the slice: x: 2, y: 2, z: 4, core: 2. Of those that a mesh axis runs over, the one named last changes fastest.
Arguments:
- orbitals: float32 [32, 100, 1024], P(('parts', 'chol')), parts along dimension 0, may hold values from -6 to 6
- intersection_inv: float32 [32, 100, 100], P(('parts', 'chol')), parts along dimension 0, may hold values from -0.625 to 0.625
- factor_rows: bfloat16 [4096, 1024], P('chol'), may hold values from -0.1875 to 0.1875
- factor_rotated: bfloat16 [100, 4096], replicated, may hold values from -0.625 to 0.625
- factor_core: bfloat16 [1024, 4096], P('chol'), may hold values from -0.125 to 0.125
- fields: float32 [32, 1024], P('parts', 'chol'), parts along dimension 0, may hold values from -6 to 6
Outputs:
- propagated: float32 [32, 100, 1024], P(('parts', 'chol')), parts along dimension 0
- force_bias: float32 [32, 1024], P('parts', 'chol'), parts along dimension 0
The draws below stay inside these ranges and needn't reach their ends.
There are 2 independent parts, one for each index of `parts`. The reference program is written for one: setup_inputs(seed, part) draws one part's arguments, and reference() takes and returns one part's arrays. A program takes and returns all parts, laid end to end along the dimension named above; an argument that names none is the same for every part. Nothing has to cross between parts.
All inputs are finite; a program needn't handle non-finite values.
Results may differ from the reference program's by a relative error of at most 0.0091.
Values may be sent and summed in bfloat16 or wider, within the bound.
A program may use at most 64 MiB of HBM per device.

```python
import jax
import jax.numpy as jnp
from jax import lax

M = 1024
NE = 100
NP = 4096
TAYLOR = 4
NCHOL = 1024
W = 16


def shard_levels(stream_key, dims, cuts, low, high):
    factor_of = 1.0
    for dim, blocks in cuts:
        draws = jax.random.uniform(jax.random.fold_in(jax.random.fold_in(stream_key, 6), dim), (blocks,), jnp.float32, low / len(cuts), high / len(cuts))
        factor_of = factor_of * jnp.repeat(jnp.exp(draws), dims[dim] // blocks).reshape((-1,) + (1,) * (len(dims) - 1 - dim))
    return factor_of


def normal_values(rng, dims, deviation, most, shards=(), held_as=jnp.bfloat16):
    level = shard_levels(rng, dims, shards, -0.22, 0.18) if shards else 1.0
    entries = jax.random.normal(rng, dims, jnp.float32) * deviation * level
    return jnp.minimum(jnp.maximum(entries, -most), most).astype(held_as)


def setup_inputs(seed: int = 0, part: int = 0) -> dict:
    keys = jax.random.split(jax.random.key(seed), 7)
    own_keys = jax.random.split(jax.random.fold_in(keys[6], part), 7)
    return {
        "orbitals": normal_values(own_keys[0], (W, NE, M), 1.0, 6.0, ((0, 16),), jnp.float32),
        "intersection_inv": normal_values(own_keys[1], (W, NE, NE), NE ** -0.5, 0.625, ((0, 16),), jnp.float32),
        "factor_rows": normal_values(keys[2], (NP, M), M ** -0.5, 0.1875, ((0, 16),)),
        "factor_rotated": normal_values(keys[3], (NE, NP), NE ** -0.5, 0.625),
        "factor_core": normal_values(keys[4], (NCHOL, NP), (NP * NCHOL // (2 * M)) ** -0.5, 0.125, ((0, 16),)),
        "fields": normal_values(own_keys[5], (W, NCHOL), 1.0, 6.0, ((1, 16),), jnp.float32),
    }


def density_one(half_green, factor_rows, factor_rotated):
    projected = lax.dot_general(half_green, factor_rows, (((1,), (1,)), ((), ())), preferred_element_type=jnp.float32)
    return jnp.sum(factor_rotated.astype(jnp.float32) * projected, axis=0).astype(jnp.bfloat16)


def propagate_one(orbital, potential, factor_rows):
    total = orbital
    term = orbital
    for order in range(1, TAYLOR + 1):
        summed = lax.dot_general(term.astype(jnp.bfloat16), factor_rows, (((1,), (1,)), ((), ())), preferred_element_type=jnp.float32)
        scaled = (summed * potential[None, :] / order).astype(jnp.bfloat16)
        term = jnp.dot(scaled, factor_rows, preferred_element_type=jnp.float32)
        total = total + term
    return total


def reference(orbitals, intersection_inv, factor_rows, factor_rotated, factor_core, fields):
    half_green = jnp.einsum("wij,wjm->wim", intersection_inv, orbitals, precision=lax.Precision.HIGHEST).astype(jnp.bfloat16)
    density = lax.map(lambda item: density_one(item, factor_rows, factor_rotated), half_green)
    force_bias = lax.dot_general(density, factor_core, (((1,), (1,)), ((), ())), preferred_element_type=jnp.float32)
    shifted = (fields - force_bias).astype(jnp.bfloat16)
    potential = jnp.dot(shifted, factor_core, preferred_element_type=jnp.float32)
    propagated = lax.map(lambda pair: propagate_one(pair[0], pair[1], factor_rows), (orbitals, potential))
    return propagated, force_bias
```

```python
import functools

import jax
import jax.numpy as jnp
from jax import lax
from jax.experimental import pallas as pl
from jax.experimental.pallas import tpu as pltpu
from jax.sharding import PartitionSpec as P

TAYLOR = 4
F32, BF16 = jnp.float32, jnp.bfloat16
LAST = (((1,), (1,)), ((), ()))


def kernel(
    n, orb_ref, inv_ref, rows_ref, rot_ref, core_ref, fields_ref, out_ref, fb_ref,
    xbuf, lhs, pad, rot, corep, s1, sc, dbuf, dfull, pbuf, rbuf, pot, tpart, tsend, trecv, tbf, total,
    own_sem, rot_sem, core_sem, ring_send, ring_recv, pair_send, pair_recv,
    dens_send, dens_recv, pot_send, pot_recv, term_send, term_recv,
):
    h = n // 2
    p, m = rows_ref.shape
    ne = orb_ref.shape[1]
    nep = pad.shape[0]
    half = h * p
    piece = p // 2
    me = lax.axis_index("chol")
    q, c = me // 2, me % 2
    partner = q * 2 + (1 - c)
    r = (1 - q % 2) * (q // 2) + (q % 2) * (h - 1 - q // 2)

    def chip_at(pos):
        pos = (pos + 2 * h) % h
        s = pos // (h // 2)
        return (1 - s) * 2 * pos + s * (2 * (h - 1 - pos) + 1)

    barrier = pltpu.get_barrier_semaphore()
    for k in range(1, n):
        pl.semaphore_signal(barrier, inc=1, device_id={"chol": (me + k) % n}, device_id_type=pl.DeviceIdType.MESH)

    own_copy = pltpu.make_async_copy(rows_ref, xbuf.at[pl.ds(pl.multiple_of(q * p, p), p)], own_sem)
    own_copy.start()
    rot_copy = pltpu.make_async_copy(rot_ref, rot, rot_sem)
    rot_copy.start()
    core_copies = []
    for s in range(n):
        copy = pltpu.make_async_copy(
            core_ref.at[:, pl.ds(s * p, p)],
            corep.at[:, pl.ds((s % 2) * half + (s // 2) * p, p)],
            core_sem.at[s],
        )
        copy.start()
        core_copies.append(copy)

    pl.semaphore_wait(barrier, n - 1)

    def remote(src, dst, send, recv, target):
        return pltpu.make_async_remote_copy(
            src_ref=src, dst_ref=dst, send_sem=send, recv_sem=recv,
            device_id={"chol": target}, device_id_type=pl.DeviceIdType.MESH,
        )

    def slot(chip, part):
        return xbuf.at[pl.ds(pl.multiple_of(chip * p + part * piece, piece), piece)]

    def hop(way, step, part):
        sign = 1 - 2 * way
        origin = chip_at(r - sign * (step - 1))
        src = rows_ref.at[pl.ds(part * piece, piece)] if step == 1 else slot(origin, part)
        return remote(
            src, slot(origin, part), ring_send.at[way, step - 1, part], ring_recv.at[way, step - 1, part],
            chip_at(r + sign) * 2 + c,
        )

    def arrival(way, step, part):
        sign = 1 - 2 * way
        here = slot(chip_at(r - sign * step), part)
        return remote(
            here, here, ring_send.at[way, step - 1, part], ring_recv.at[way, step - 1, part], chip_at(r + sign) * 2 + c
        )

    def travels(way, step, part):
        return step < h // 2 or (step == h // 2 and part == way)

    sent = []
    for part in range(2):
        for way in range(2):
            if travels(way, 1, part):
                copy = hop(way, 1, part)
                copy.start()
                sent.append(copy)

    own_walker = orb_ref[0]
    pad[...] = jnp.zeros_like(pad)
    pad[0:ne] = own_walker
    total[...] = pad[...]
    lhs[c, nep : 2 * nep] = pad[...].astype(BF16)
    pad[0:ne] = jnp.dot(inv_ref[0], own_walker, preferred_element_type=F32, precision=lax.Precision.HIGHEST)
    lhs[c, 0:nep] = pad[...].astype(BF16)
    pair = remote(lhs.at[c], lhs.at[c], pair_send, pair_recv, partner)
    pair.start()
    sent.append(pair)
    own_copy.wait()
    rot_copy.wait()
    remote(lhs.at[1 - c], lhs.at[1 - c], pair_send, pair_recv, partner).wait_recv()

    def block(chip):
        where = pl.ds(pl.multiple_of(chip * p, p), p)
        result = lax.dot_general(
            lhs[...].reshape(4 * nep, m), xbuf[where, :], LAST, preferred_element_type=F32
        )
        rotated = rot[:, pl.ds(pl.multiple_of((chip * 2 + c) * p, p), p)].astype(F32)
        for w in range(2):
            projected = result[w * 2 * nep : w * 2 * nep + ne]
            density = jnp.sum(rotated * projected, axis=0, keepdims=True)
            dbuf[me, w : w + 1, where] = density.astype(BF16).astype(F32)
            s1[w * nep : (w + 1) * nep, where] = result[w * 2 * nep + nep : (w + 1) * 2 * nep]

    block(q)
    for step in range(1, h // 2 + 1):
        for part in range(2):
            for way in range(2):
                if travels(way, step, part):
                    arrival(way, step, part).wait_recv()
                    if travels(way, step + 1, part):
                        copy = hop(way, step + 1, part)
                        copy.start()
                        sent.append(copy)
        block(chip_at(r - step))
        if step < h // 2:
            block(chip_at(r + step))

    for k in range(1, n):
        copy = remote(dbuf.at[me], dbuf.at[me], dens_send.at[k - 1], dens_recv.at[k - 1], (me + k) % n)
        copy.start()
        sent.append(copy)
    for copy in core_copies:
        copy.wait()
    for k in range(1, n):
        source = (me + n - k) % n
        remote(dbuf.at[source], dbuf.at[source], dens_send.at[k - 1], dens_recv.at[k - 1], source).wait_recv()
    for s in range(n):
        dfull[2 * (s // 2) : 2 * (s // 2) + 2, (s % 2) * half : (s % 2 + 1) * half] = dbuf[s]
    force_bias = lax.dot_general(dfull[...].astype(BF16), corep[...], LAST, preferred_element_type=F32)
    fb_ref[...] = force_bias
    shifted = (fields_ref[...] - force_bias).astype(BF16)
    for side in range(2):
        dfull[:, side * half : (side + 1) * half] = jnp.dot(
            shifted, corep[:, side * half : (side + 1) * half], preferred_element_type=F32
        )
    for s in range(n):
        pbuf[s] = dfull[2 * (s // 2) : 2 * (s // 2) + 2, (s % 2) * half : (s % 2 + 1) * half]
    for k in range(1, n):
        target = (me + k) % n
        copy = remote(pbuf.at[target], rbuf.at[k - 1], pot_send.at[k - 1], pot_recv.at[k - 1], target)
        copy.start()
        sent.append(copy)
    summed = pbuf[me]
    for k in range(1, n):
        remote(rbuf.at[k - 1], rbuf.at[k - 1], pot_send.at[k - 1], pot_recv.at[k - 1], partner).wait_recv()
        summed = summed + rbuf[k - 1]
    pot[...] = summed

    wide = tpart.shape[2]
    for order in range(1, TAYLOR + 1):
        for j in range(h):
            where = slice(j * p, (j + 1) * p)
            if order == 1:
                result = s1[:, where]
            else:
                result = lax.dot_general(tbf[...], xbuf[where, :], LAST, preferred_element_type=F32)
            for w in range(2):
                scale = pot[w : w + 1, where] / order
                sc[w * nep : (w + 1) * nep, where] = (result[w * nep : (w + 1) * nep] * scale).astype(BF16)
        last = order == TAYLOR
        for j in range(m // wide):
            result = jnp.dot(sc[...], xbuf[:, j * wide : (j + 1) * wide], preferred_element_type=F32)
            tpart[j] = result
            tsend[order - 1, j] = result.astype(BF16)
            mine = pl.ds(pl.multiple_of((1 - c) * nep, nep), nep) if last else pl.ds(0, 2 * nep)
            view = (order - 1, j, mine)
            copy = remote(
                tsend.at[view], trecv.at[view], term_send.at[order - 1, j], term_recv.at[order - 1, j], partner
            )
            copy.start()
            sent.append(copy)
        own = pl.ds(pl.multiple_of(c * nep, nep), nep)
        for j in range(m // wide):
            where = slice(j * wide, (j + 1) * wide)
            mine = own if last else pl.ds(0, 2 * nep)
            view = trecv.at[order - 1, j, mine]
            remote(view, view, term_send.at[order - 1, j], term_recv.at[order - 1, j], partner).wait_recv()
            total[:, where] += tpart[j, own] + trecv[order - 1, j, own].astype(F32)
            if not last:
                tbf[:, where] = (tpart[j] + trecv[order - 1, j].astype(F32)).astype(BF16)
    out_ref[0] = total[0:ne]
    for copy in sent:
        copy.wait_send()


def fused(orbitals, intersection_inv, factor_rows, factor_rotated, factor_core, fields, n):
    h = n // 2
    p, m = factor_rows.shape
    ne, points = factor_rotated.shape
    nep = -(-ne // 16) * 16
    half = h * p
    walkers = fields.shape[0]
    wide = 256
    vmem = pl.BlockSpec(memory_space=pltpu.VMEM)
    hbm = pl.BlockSpec(memory_space=pl.ANY)
    dma = pltpu.SemaphoreType.DMA
    return pl.pallas_call(
        functools.partial(kernel, n),
        out_shape=(
            jax.ShapeDtypeStruct(orbitals.shape, F32),
            jax.ShapeDtypeStruct(fields.shape, F32),
        ),
        in_specs=[vmem, vmem, hbm, hbm, hbm, vmem],
        out_specs=(vmem, vmem),
        scratch_shapes=[
            pltpu.VMEM((half, m), BF16),
            pltpu.VMEM((2, 2 * nep, m), BF16),
            pltpu.VMEM((nep, m), F32),
            pltpu.VMEM((ne, points), BF16),
            pltpu.VMEM(factor_core.shape, BF16),
            pltpu.VMEM((2 * nep, half), F32),
            pltpu.VMEM((2 * nep, half), BF16),
            pltpu.VMEM((n, 2, half), F32),
            pltpu.VMEM((walkers, points), F32),
            pltpu.VMEM((n, 2, half), F32),
            pltpu.VMEM((n - 1, 2, half), F32),
            pltpu.VMEM((2, half), F32),
            pltpu.VMEM((m // wide, 2 * nep, wide), F32),
            pltpu.VMEM((TAYLOR, m // wide, 2 * nep, wide), BF16),
            pltpu.VMEM((TAYLOR, m // wide, 2 * nep, wide), BF16),
            pltpu.VMEM((2 * nep, m), BF16),
            pltpu.VMEM((nep, m), F32),
            dma(()),
            dma(()),
            dma((n,)),
            dma((2, h // 2, 2)),
            dma((2, h // 2, 2)),
            dma(()),
            dma(()),
            dma((n - 1,)),
            dma((n - 1,)),
            dma((n - 1,)),
            dma((n - 1,)),
            dma((TAYLOR, m // wide)),
            dma((TAYLOR, m // wide)),
        ],
        compiler_params=pltpu.CompilerParams(
            collective_id=0, has_side_effects=True, vmem_limit_bytes=56 * 1024 * 1024
        ),
    )(orbitals, intersection_inv, factor_rows, factor_rotated, factor_core, fields)


def density_one(half_green, all_rows, factor_rotated):
    projected = lax.dot_general(half_green, all_rows, LAST, preferred_element_type=F32)
    return jnp.sum(factor_rotated.astype(F32) * projected, axis=0).astype(BF16)


def propagate_one(orbital, potential, all_rows):
    total = orbital
    term = orbital
    for order in range(1, TAYLOR + 1):
        summed = lax.dot_general(term.astype(BF16), all_rows, LAST, preferred_element_type=F32)
        scaled = (summed * potential[None, :] / order).astype(BF16)
        term = jnp.dot(scaled, all_rows, preferred_element_type=F32)
        total = total + term
    return total


def plain(orbitals, intersection_inv, factor_rows, factor_rotated, factor_core, fields):
    walker_count = orbitals.shape[0]
    half_green = jnp.einsum(
        "wij,wjm->wim", intersection_inv, orbitals, precision=lax.Precision.HIGHEST
    ).astype(BF16)
    all_rows = lax.all_gather(factor_rows, "chol", axis=0, tiled=True)
    own_density = lax.map(lambda item: density_one(item, all_rows, factor_rotated), half_green)
    density = lax.all_gather(own_density, "chol", axis=0, tiled=True)
    force_bias = lax.dot_general(density, factor_core, LAST, preferred_element_type=F32)
    shifted = (fields - force_bias).astype(BF16)
    partial_sum = jnp.dot(shifted, factor_core, preferred_element_type=F32)
    summed_all = lax.psum(partial_sum, "chol")
    potential = lax.dynamic_slice_in_dim(
        summed_all, lax.axis_index("chol") * walker_count, walker_count, 0
    )
    propagated = lax.map(lambda pair: propagate_one(pair[0], pair[1], all_rows), (orbitals, potential))
    return (propagated, force_bias)


def solution(mesh):
    n = mesh.shape["chol"]

    def on_device(orbitals, intersection_inv, factor_rows, factor_rotated, factor_core, fields):
        args = (orbitals, intersection_inv, factor_rows, factor_rotated, factor_core, fields)
        rows, m = factor_rows.shape
        if orbitals.shape[0] == 1 and n % 4 == 0 and rows % 256 == 0 and m % 256 == 0:
            return fused(*args, n)
        return plain(*args)

    in_specs = (
        P(("parts", "chol"), None, None),
        P(("parts", "chol"), None, None),
        P("chol", None),
        P(),
        P("chol", None),
        P("parts", "chol"),
    )
    out_specs = (P(("parts", "chol"), None, None), P("parts", "chol"))
    return jax.shard_map(
        on_device, mesh=mesh, in_specs=in_specs, out_specs=out_specs, check_vma=False
    )
```

```python
import functools

import jax
import jax.numpy as jnp
from jax import lax
from jax.experimental import pallas as pl
from jax.experimental.pallas import tpu as pltpu
from jax.sharding import PartitionSpec as P

TAYLOR = 4
F32, BF16 = jnp.float32, jnp.bfloat16
LAST = (((1,), (1,)), ((), ()))


def kernel(
    n, orb_ref, inv_ref, rows_ref, rot_ref, core_ref, fields_ref, out_ref, fb_ref,
    xbuf, orb3, lhs, pad, rot, corep, s1, sc, dbuf, dfull, pbuf, rbuf, pot, tpart, tsend, trecv, tbf, total,
    orb_sem, own_sem, rot_sem, core_sem, ring_send, ring_recv, twin_send, twin_recv, pair_send, pair_recv,
    dens_send, dens_recv, ready_sem, pot_send, pot_recv, term_send, term_recv,
):
    h = n // 2
    p, m = rows_ref.shape
    ne = orb_ref.shape[0]
    nep = pad.shape[0]
    half = h * p
    side_rows = p * 5 // 256 * 16
    sizes = (side_rows, p - 2 * side_rows)
    here = lax.axis_index("parts")
    starts = (here * side_rows, 2 * side_rows)
    me = lax.axis_index("chol")
    q, c = me // 2, me % 2
    partner = q * 2 + (1 - c)
    r = (1 - q % 2) * (q // 2) + (q % 2) * (h - 1 - q // 2)

    def chip_at(pos):
        pos = (pos + 2 * h) % h
        s = pos // (h // 2)
        return (1 - s) * 2 * pos + s * (2 * (h - 1 - pos) + 1)

    barrier = pltpu.get_barrier_semaphore()
    for near in (partner, chip_at(r + 1) * 2 + c, chip_at(r - 1) * 2 + c):
        pl.semaphore_signal(barrier, inc=1, device_id={"chol": near}, device_id_type=pl.DeviceIdType.MESH)
    pl.semaphore_signal(barrier, inc=1, device_id={"parts": 1 - here}, device_id_type=pl.DeviceIdType.MESH)

    orb_copy = pltpu.make_async_copy(orb_ref, orb3, orb_sem)
    orb_copy.start()
    own_copy = pltpu.make_async_copy(rows_ref, xbuf.at[pl.ds(pl.multiple_of(q * p, p), p)], own_sem)
    own_copy.start()
    rot_copy = pltpu.make_async_copy(rot_ref, rot, rot_sem)
    rot_copy.start()
    core_copies = []
    for s in range(n):
        copy = pltpu.make_async_copy(
            core_ref.at[:, pl.ds(s * p, p)],
            corep.at[:, pl.ds((s % 2) * half + (s // 2) * p, p)],
            core_sem.at[s],
        )
        copy.start()
        core_copies.append(copy)

    pl.semaphore_wait(barrier, 4)

    def remote(src, dst, send, recv, target):
        return pltpu.make_async_remote_copy(
            src_ref=src, dst_ref=dst, send_sem=send, recv_sem=recv,
            device_id={"chol": target}, device_id_type=pl.DeviceIdType.MESH,
        )

    def rows(way, step, part):
        if step < h // 2:
            return pl.multiple_of(starts[part], 16), sizes[part]
        if part == 1:
            return 2 * side_rows + way * (sizes[1] // 2), sizes[1] // 2
        return pl.multiple_of((way + (1 - 2 * way) * here) * side_rows, 16), side_rows

    def slot(chip, way, step, part):
        first, size = rows(way, step, part)
        return xbuf.at[pl.ds(pl.multiple_of(chip * p + first, 16), size)]

    def twin(way, step, row):
        view = xbuf.at[pl.ds(pl.multiple_of(chip_at(r - (1 - 2 * way) * step) * p + row, 16), side_rows)]
        return pltpu.make_async_remote_copy(
            src_ref=view, dst_ref=view, send_sem=twin_send.at[way, step - 1], recv_sem=twin_recv.at[way, step - 1],
            device_id={"parts": 1 - here}, device_id_type=pl.DeviceIdType.MESH,
        )

    def hop(way, step, part):
        sign = 1 - 2 * way
        origin = chip_at(r - sign * (step - 1))
        src = rows_ref.at[pl.ds(*rows(way, step, part))] if step == 1 else slot(origin, way, step, part)
        return remote(
            src, slot(origin, way, step, part), ring_send.at[way, step - 1, part], ring_recv.at[way, step - 1, part],
            chip_at(r + sign) * 2 + c,
        )

    def arrival(way, step, part):
        sign = 1 - 2 * way
        landed = slot(chip_at(r - sign * step), way, step, part)
        return remote(
            landed, landed, ring_send.at[way, step - 1, part], ring_recv.at[way, step - 1, part],
            chip_at(r + sign) * 2 + c,
        )

    sent = []
    for part in range(2):
        for way in range(2):
            copy = hop(way, 1, part)
            copy.start()
            sent.append(copy)

    pad[...] = jnp.zeros_like(pad)
    orb_copy.wait()
    for j in range(m // 128):
        pad[0:ne, j * 128 : (j + 1) * 128] = orb3[:, j]
    total[...] = pad[...]
    lhs[c, nep : 2 * nep] = pad[...].astype(BF16)
    pad[0:ne] = jnp.dot(inv_ref[0], pad[0:ne], preferred_element_type=F32, precision=lax.Precision.HIGHEST)
    lhs[c, 0:nep] = pad[...].astype(BF16)
    pair = remote(lhs.at[c], lhs.at[c], pair_send, pair_recv, partner)
    pair.start()
    sent.append(pair)
    own_copy.wait()
    rot_copy.wait()
    remote(lhs.at[1 - c], lhs.at[1 - c], pair_send, pair_recv, partner).wait_recv()

    def block(chip, place):
        where = pl.ds(pl.multiple_of(chip * p, p), p)
        result = lax.dot_general(
            lhs[...].reshape(4 * nep, m), xbuf[where, :], LAST, preferred_element_type=F32
        )
        rotated = rot[:, pl.ds(pl.multiple_of((chip * 2 + c) * p, p), p)].astype(F32)
        for w in range(2):
            projected = result[w * 2 * nep : w * 2 * nep + ne]
            density = jnp.sum(rotated * projected, axis=0, keepdims=True)
            dbuf[me, w : w + 1, place * p : (place + 1) * p] = density.astype(BF16).astype(F32)
            s1[w * nep : (w + 1) * nep, where] = result[w * 2 * nep + nep : (w + 1) * 2 * nep]

    def finish(step):
        if step < h // 2:
            for way in range(2 if step < h // 2 - 1 else 1):
                twin(way, step, (1 - here) * side_rows).wait_recv()
            block(chip_at(r - step), 2 * step - 1)
            block(chip_at(r + step), 2 * step)
        else:
            block(chip_at(r - step), h - 1)

    cut = (h - 1) * p
    spans = (pl.ds(0, cut), pl.ds(cut, p))

    def spread(group):
        for k in range(1, n):
            view = dbuf.at[me, :, spans[group]]
            copy = remote(view, view, dens_send.at[group, k - 1], dens_recv.at[group, k - 1], (me + k) % n)
            copy.start()
            sent.append(copy)

    block(q, 0)
    for step in range(1, h // 2 + 1):
        for part in range(2):
            for way in (1, 0):
                arrival(way, step, part).wait_recv()
                if step < h // 2 - 1 or (step == h // 2 - 1 and (way, part) != (1, 0)):
                    copy = hop(way, step + 1, part)
                    copy.start()
                    sent.append(copy)
                if part == 0 and step < h // 2:
                    copy = twin(way, step, here * side_rows)
                    copy.start()
                    sent.append(copy)
        if step == h // 2:
            pl.semaphore_signal(ready_sem, inc=1, device_id={"chol": partner}, device_id_type=pl.DeviceIdType.MESH)
        if step > 1:
            finish(step - 1)
        if step == h // 2 - 1:
            twin(1, step, (1 - here) * side_rows).wait_recv()
            copy = hop(1, step + 1, 0)
            copy.start()
            sent.append(copy)
    pl.semaphore_wait(ready_sem, 1)
    spread(0)
    finish(h // 2)
    spread(1)
    for copy in core_copies:
        copy.wait()
    for group in range(2):
        for k in range(1, n):
            source = (me + n - k) % n
            view = dbuf.at[source, :, spans[group]]
            remote(view, view, dens_send.at[group, k - 1], dens_recv.at[group, k - 1], source).wait_recv()
    for s in range(n):
        chip, side = s // 2, s % 2
        pos = chip // 2 if chip % 2 == 0 else h - 1 - chip // 2
        for place in range(h):
            step = (place + 1) // 2
            other = chip_at(pos - step if place % 2 else pos + step)
            first = side * half + other * p
            dfull[2 * chip : 2 * chip + 2, first : first + p] = dbuf[s, :, place * p : (place + 1) * p]
    force_bias = lax.dot_general(dfull[...].astype(BF16), corep[...], LAST, preferred_element_type=F32)
    fb_ref[...] = force_bias
    shifted = (fields_ref[...] - force_bias).astype(BF16)
    for side in range(2):
        dfull[:, side * half : (side + 1) * half] = jnp.dot(
            shifted, corep[:, side * half : (side + 1) * half], preferred_element_type=F32
        )
    for s in range(n):
        pbuf[s] = dfull[2 * (s // 2) : 2 * (s // 2) + 2, (s % 2) * half : (s % 2 + 1) * half]
    for k in range(1, n):
        target = (me + k) % n
        copy = remote(pbuf.at[target], rbuf.at[k - 1], pot_send.at[k - 1], pot_recv.at[k - 1], target)
        copy.start()
        sent.append(copy)
    summed = pbuf[me]
    for k in range(1, n):
        remote(rbuf.at[k - 1], rbuf.at[k - 1], pot_send.at[k - 1], pot_recv.at[k - 1], partner).wait_recv()
        summed = summed + rbuf[k - 1]
    pot[...] = summed

    wide = tpart.shape[2]
    for order in range(1, TAYLOR + 1):
        for j in range(h):
            where = slice(j * p, (j + 1) * p)
            if order == 1:
                result = s1[:, where]
            else:
                result = lax.dot_general(tbf[...], xbuf[where, :], LAST, preferred_element_type=F32)
            for w in range(2):
                scale = pot[w : w + 1, where] / order
                sc[w * nep : (w + 1) * nep, where] = (result[w * nep : (w + 1) * nep] * scale).astype(BF16)
        last = order == TAYLOR
        for j in range(m // wide):
            result = jnp.dot(sc[...], xbuf[:, j * wide : (j + 1) * wide], preferred_element_type=F32)
            tpart[j] = result
            tsend[order - 1, j] = result.astype(BF16)
            mine = pl.ds(pl.multiple_of((1 - c) * nep, nep), nep) if last else pl.ds(0, 2 * nep)
            view = (order - 1, j, mine)
            copy = remote(
                tsend.at[view], trecv.at[view], term_send.at[order - 1, j], term_recv.at[order - 1, j], partner
            )
            copy.start()
            sent.append(copy)
        own = pl.ds(pl.multiple_of(c * nep, nep), nep)
        for j in range(m // wide):
            where = slice(j * wide, (j + 1) * wide)
            mine = own if last else pl.ds(0, 2 * nep)
            view = trecv.at[order - 1, j, mine]
            remote(view, view, term_send.at[order - 1, j], term_recv.at[order - 1, j], partner).wait_recv()
            total[:, where] += tpart[j, own] + trecv[order - 1, j, own].astype(F32)
            if not last:
                tbf[:, where] = (tpart[j] + trecv[order - 1, j].astype(F32)).astype(BF16)
    for j in range(m // 128):
        out_ref[:, j] = total[0:ne, j * 128 : (j + 1) * 128]
    for copy in sent:
        copy.wait_send()


def fused(orbitals, intersection_inv, factor_rows, factor_rotated, factor_core, fields, n):
    h = n // 2
    p, m = factor_rows.shape
    ne, points = factor_rotated.shape
    nep = -(-ne // 16) * 16
    half = h * p
    walkers = fields.shape[0]
    wide = 256
    vmem = pl.BlockSpec(memory_space=pltpu.VMEM)
    hbm = pl.BlockSpec(memory_space=pl.ANY)
    dma = pltpu.SemaphoreType.DMA
    propagated, force_bias = pl.pallas_call(
        functools.partial(kernel, n),
        out_shape=(
            jax.ShapeDtypeStruct((ne, m // 128, 128), F32),
            jax.ShapeDtypeStruct(fields.shape, F32),
        ),
        in_specs=[hbm, vmem, hbm, hbm, hbm, vmem],
        out_specs=(vmem, vmem),
        scratch_shapes=[
            pltpu.VMEM((half, m), BF16),
            pltpu.VMEM((ne, m // 128, 128), F32),
            pltpu.VMEM((2, 2 * nep, m), BF16),
            pltpu.VMEM((nep, m), F32),
            pltpu.VMEM((ne, points), BF16),
            pltpu.VMEM(factor_core.shape, BF16),
            pltpu.VMEM((2 * nep, half), F32),
            pltpu.VMEM((2 * nep, half), BF16),
            pltpu.VMEM((n, 2, half), F32),
            pltpu.VMEM((walkers, points), F32),
            pltpu.VMEM((n, 2, half), F32),
            pltpu.VMEM((n - 1, 2, half), F32),
            pltpu.VMEM((2, half), F32),
            pltpu.VMEM((m // wide, 2 * nep, wide), F32),
            pltpu.VMEM((TAYLOR, m // wide, 2 * nep, wide), BF16),
            pltpu.VMEM((TAYLOR, m // wide, 2 * nep, wide), BF16),
            pltpu.VMEM((2 * nep, m), BF16),
            pltpu.VMEM((nep, m), F32),
            dma(()),
            dma(()),
            dma(()),
            dma((n,)),
            dma((2, h // 2, 2)),
            dma((2, h // 2, 2)),
            dma((2, h // 2)),
            dma((2, h // 2)),
            dma(()),
            dma(()),
            dma((2, n - 1)),
            dma((2, n - 1)),
            pltpu.SemaphoreType.REGULAR,
            dma((n - 1,)),
            dma((n - 1,)),
            dma((TAYLOR, m // wide)),
            dma((TAYLOR, m // wide)),
        ],
        compiler_params=pltpu.CompilerParams(
            collective_id=0, has_side_effects=True, vmem_limit_bytes=56 * 1024 * 1024
        ),
    )(orbitals.reshape(ne, m // 128, 128), intersection_inv, factor_rows, factor_rotated, factor_core, fields)
    return propagated.reshape(orbitals.shape), force_bias


def density_one(half_green, all_rows, factor_rotated):
    projected = lax.dot_general(half_green, all_rows, LAST, preferred_element_type=F32)
    return jnp.sum(factor_rotated.astype(F32) * projected, axis=0).astype(BF16)


def propagate_one(orbital, potential, all_rows):
    total = orbital
    term = orbital
    for order in range(1, TAYLOR + 1):
        summed = lax.dot_general(term.astype(BF16), all_rows, LAST, preferred_element_type=F32)
        scaled = (summed * potential[None, :] / order).astype(BF16)
        term = jnp.dot(scaled, all_rows, preferred_element_type=F32)
        total = total + term
    return total


def plain(orbitals, intersection_inv, factor_rows, factor_rotated, factor_core, fields):
    walker_count = orbitals.shape[0]
    half_green = jnp.einsum(
        "wij,wjm->wim", intersection_inv, orbitals, precision=lax.Precision.HIGHEST
    ).astype(BF16)
    all_rows = lax.all_gather(factor_rows, "chol", axis=0, tiled=True)
    own_density = lax.map(lambda item: density_one(item, all_rows, factor_rotated), half_green)
    density = lax.all_gather(own_density, "chol", axis=0, tiled=True)
    force_bias = lax.dot_general(density, factor_core, LAST, preferred_element_type=F32)
    shifted = (fields - force_bias).astype(BF16)
    partial_sum = jnp.dot(shifted, factor_core, preferred_element_type=F32)
    summed_all = lax.psum(partial_sum, "chol")
    potential = lax.dynamic_slice_in_dim(
        summed_all, lax.axis_index("chol") * walker_count, walker_count, 0
    )
    propagated = lax.map(lambda pair: propagate_one(pair[0], pair[1], all_rows), (orbitals, potential))
    return (propagated, force_bias)


def solution(mesh):
    n = mesh.shape["chol"]

    def on_device(orbitals, intersection_inv, factor_rows, factor_rotated, factor_core, fields):
        args = (orbitals, intersection_inv, factor_rows, factor_rotated, factor_core, fields)
        rows, m = factor_rows.shape
        if orbitals.shape[0] == 1 and n % 4 == 0 and n > 8 and rows % 256 == 0 and mesh.shape["parts"] == 2 and m % 256 == 0:
            return fused(*args, n)
        return plain(*args)

    in_specs = (
        P(("parts", "chol"), None, None),
        P(("parts", "chol"), None, None),
        P("chol", None),
        P(),
        P("chol", None),
        P("parts", "chol"),
    )
    out_specs = (P(("parts", "chol"), None, None), P("parts", "chol"))
    return jax.shard_map(
        on_device, mesh=mesh, in_specs=in_specs, out_specs=out_specs, check_vma=False
    )
```
